32 devices in a mesh: grp: 2 (over y), slab: 2 (over x), lat: 8 (over z, core).
Axes of the slice: x: 2, y: 2, z: 4, core: 2. Of those that a mesh axis runs over, the one named last changes fastest.
Arguments:
- cond_lists: int32 [64, 16], P(('slab', 'lat')), may hold values from 0 to 31, all different within a row
- regress: float32 [64, 128, 2048], P(('slab', 'lat')), may hold values from -0.09375 to 0.09375
- chol: float32 [64, 128, 128], P(('slab', 'lat')), as said below
- noise: float32 [128, 256, 128], P(('grp', 'slab', 'lat')), parts along dimension 0, may hold values from -6 to 6
- start_field: float32 [64, 256, 128], P(('grp', 'lat')), parts along dimension 0, may hold values from -6 to 6
Outputs:
- field: float32 [128, 256, 128], P(('grp', 'slab', 'lat')), parts along dimension 0
The draws below stay inside these ranges and needn't reach their ends.
There are 2 independent parts, one for each index of `grp`. The reference program is written for one: setup_inputs(seed, part) draws one part's arguments, and reference() takes and returns one part's arrays. A program takes and returns all parts, laid end to end along the dimension named above; an argument that names none is the same for every part. Nothing has to cross between parts.
Inputs may be any that keep to these rules, and one draw needn't show every extreme that they name: `cond_lists`: each row names 16 distinct positions of the previous slab. `chol`: each factor is lower triangular with diagonal entries from 0.3 to 0.7.
All inputs are finite; a program needn't handle non-finite values.
Results may differ from the reference program's by a relative error of at most 0.0001.
Values sent between devices are 32-bit elements; how exact they have to be, the bound alone decides.
No kernel may reach another device: no remote copies, remote signals or barrier semaphores. Data moves between devices by JAX's collectives and lax.ppermute only.
A program may use at most 64 MiB of HBM per device.

```python
import math
import jax
import jax.numpy as jnp
from jax import lax

B = 128
K = 16
BD = 4
NREAL = 256
NBLK = 64
N_SLAB = 2
N_LAT = 8


def draw_chol(key, part):
    off_key = jax.random.fold_in(key, 11)
    diag_key = jax.random.fold_in(key, 23)
    row_index = jnp.arange(B)
    below_mask = (row_index[:, None] > row_index[None, :]).astype(jnp.float32)
    spread = jax.random.normal(off_key, (NBLK, B, B), jnp.float32)
    diagonal = jax.random.uniform(diag_key, (NBLK, B), jnp.float32, 0.3, 0.7)
    return spread * below_mask / math.sqrt(2.0 * B) + diagonal[:, :, None] * jnp.eye(B, dtype=jnp.float32)


def steps_of(own_key, shape, split, least, high):
    def one(axis_at, blocks):
        heights = jax.random.uniform(jax.random.fold_in(jax.random.fold_in(own_key, 6), axis_at), (blocks,), jnp.float32, least / len(split), high / len(split))
        return jnp.repeat(jnp.exp(heights), shape[axis_at] // blocks).reshape((-1,) + (1,) * (len(shape) - axis_at - 1))

    level = one(*split[0])
    for cut in split[1:]:
        level = level * one(*cut)
    return level


def picks_of(key, rows, count, top, lift):
    ranking = jax.random.permutation(jax.random.fold_in(key, 1), count)
    pull = ranking
    for power in range(3):
        pull = pull * pull // count
    pull = pull * lift // count
    chance = jax.random.randint(jax.random.fold_in(key, 2), (rows, count), 0, 4096) + pull
    holders = jax.random.permutation(jax.random.fold_in(key, 3), rows)[jnp.arange(count) % rows]
    chance = jnp.where(jnp.arange(rows)[:, None] == holders[None, :], 1 << 14, chance)
    merit = chance * count + jnp.arange(count)
    return lax.top_k(merit.astype(jnp.int32), top)[1].astype(jnp.int32)


def centred(own_key, extent, scale, limit, shards=(), kind=jnp.bfloat16):
    drawn = scale * jax.random.normal(own_key, extent, jnp.float32)
    if shards:
        drawn = drawn * steps_of(own_key, extent, shards, -0.22, 0.18)
    return jnp.clip(drawn, -limit, limit).astype(kind)


def setup_inputs(seed: int = 0, part: int = 0) -> dict:
    key_list = jax.random.split(jax.random.key(seed), 6)
    part_splits = jax.random.split(jax.random.fold_in(key_list[5], part), 6)
    cond_lists = picks_of(key_list[0], NBLK, N_LAT * BD, K, 8192)
    regress = centred(key_list[1], (NBLK, B, K * B), (2 * K * B) ** -0.5, 0.09375, ((0, 16),), jnp.float32)
    chol = draw_chol(jax.random.fold_in(key_list[5], 71), part)
    noise = centred(part_splits[3], (NBLK, NREAL, B), 1.0, 6.0, ((0, 16),), jnp.float32)
    start_field = centred(part_splits[4], (N_LAT * BD, NREAL, B), 1.0, 6.0, ((0, 8),), jnp.float32)
    return dict(cond_lists=cond_lists, regress=regress, chol=chol, noise=noise, start_field=start_field)


def reference(cond_lists, regress, chol, noise, start_field):
    per_slab = N_LAT * BD
    previous = start_field
    pieces = []
    for slab_step in range(N_SLAB):
        lower_edge = slab_step * per_slab
        lists_here = cond_lists[lower_edge:lower_edge + per_slab]
        factors = regress[lower_edge:lower_edge + per_slab].reshape(per_slab, B, K, B)
        picked = previous[lists_here]
        mean_part = jnp.einsum("jakb,jkwb->jwa", factors, picked, precision=lax.Precision.HIGHEST)
        shock_part = jnp.einsum("jab,jwb->jwa", chol[lower_edge:lower_edge + per_slab], noise[lower_edge:lower_edge + per_slab], precision=lax.Precision.HIGHEST)
        fresh_blocks = mean_part + shock_part
        pieces.append(fresh_blocks)
        previous = fresh_blocks
    return jnp.concatenate(pieces, 0)
```

```python
import functools

import jax
import jax.numpy as jnp
from jax import lax
from jax.experimental import pallas as pl
from jax.experimental.pallas import tpu as pltpu
from jax.sharding import PartitionSpec as P


def general(cond_lists, regress, chol, noise, start_field):
    blocks, nreal_here, block_size = noise.shape
    list_length = cond_lists.shape[1]
    n_slab = lax.axis_size("slab")
    slab_pos = lax.axis_index("slab")
    factors = regress.reshape(blocks, block_size, list_length, block_size)
    shock = jnp.einsum("jab,jwb->jwa", chol, noise, precision=lax.Precision.HIGHEST)

    def step(at, carry):
        source, out = carry
        previous = lax.all_gather(source, "lat", axis=0, tiled=True)
        mean = jnp.einsum("jakb,jkwb->jwa", factors, previous[cond_lists], precision=lax.Precision.HIGHEST)
        fresh = mean + shock
        out = jnp.where(at == slab_pos, fresh, out)
        source = lax.ppermute(fresh, "slab", [(i, i + 1) for i in range(n_slab - 1)])
        return source, out

    return lax.fori_loop(0, n_slab, step, (start_field, jnp.zeros_like(noise)))[1]


def weights(rows, regress, blocks_all, first, earlier=None):
    blocks, size, width = regress.shape
    count = width // size
    places = 4 * blocks_all

    def kernel(rows_ref, regress_ref, *refs):
        high_ref, low_ref = refs[-2:]
        block = pl.program_id(0)
        high_ref[...] = jnp.zeros_like(high_ref)
        low_ref[...] = jnp.zeros_like(low_ref)

        def one(k, carry):
            turned = regress_ref[0, :, pl.ds(pl.multiple_of(k * size, size), size)].T
            high = turned.astype(jnp.bfloat16)
            row = rows_ref[block * count + k]
            high_ref[row] = high
            low_ref[row] = (turned - high.astype(jnp.float32)).astype(jnp.bfloat16)
            return carry

        lax.fori_loop(0, count, one, 0)

    shape = jax.ShapeDtypeStruct((places, size, blocks_all * size), jnp.bfloat16)
    spec = pl.BlockSpec((places, size, size), lambda g, rows_ref: (0, 0, first + g))
    extra = () if earlier is None else tuple(earlier)
    return pl.pallas_call(
        kernel,
        out_shape=(shape, shape),
        grid_spec=pltpu.PrefetchScalarGridSpec(
            num_scalar_prefetch=1,
            grid=(blocks,),
            in_specs=[pl.BlockSpec((1, size, width), lambda g, rows_ref: (g, 0, 0))] + [pl.BlockSpec(memory_space=pl.ANY)] * len(extra),
            out_specs=(spec, spec),
        ),
        input_output_aliases={2 + i: i for i in range(len(extra))},
        name="weights" if earlier is None else "weights_more",
    )(rows, regress, *extra)


def added(base, pieces, slots, parts):
    blocks, front, size = base.shape
    per_step = 2 if blocks % 2 == 0 else 1

    def kernel(base_ref, *refs):
        n = len(pieces)
        out_ref = refs[-1]
        total = jnp.concatenate([base_ref[i] for i in range(per_step)], axis=1)
        for i in range(n):
            piece = jnp.concatenate([refs[i][p] for p in range(blocks)], axis=1)
            high = piece.astype(jnp.bfloat16)
            low = (piece - high.astype(jnp.float32)).astype(jnp.bfloat16)
            w_high = refs[n + 2 * i][...].reshape(blocks * size, per_step * size)
            w_low = refs[n + 2 * i + 1][...].reshape(blocks * size, per_step * size)
            both = jnp.dot(jnp.concatenate([high, low], axis=0), w_high, preferred_element_type=jnp.float32)
            total = total + (both[:front] + both[front:] + jnp.dot(high, w_low, preferred_element_type=jnp.float32))
        for i in range(per_step):
            out_ref[i] = total[:, i * size:(i + 1) * size]

    block_spec = pl.BlockSpec((per_step, front, size), lambda n: (n, 0, 0))
    whole_spec = pl.BlockSpec((blocks, front, size), lambda n: (0, 0, 0))
    w_specs = []
    for slot in slots:
        w_specs += [pl.BlockSpec((blocks, size, per_step * size), functools.partial(lambda slot, n: (slot, 0, n), slot))] * 2
    return pl.pallas_call(
        kernel,
        out_shape=jax.ShapeDtypeStruct(base.shape, jnp.float32),
        grid=(blocks // per_step,),
        in_specs=[block_spec] + [whole_spec] * len(pieces) + w_specs,
        out_specs=block_spec,
        name="added%d" % len(pieces),
    )(base, *pieces, *(parts * len(pieces)))


def paired(cond_lists, regress, chol, noise, start_field):
    blocks, nreal, size = noise.shape
    half, quarter = nreal // 2, nreal // 4
    slab = lax.axis_index("slab")
    lat = lax.axis_index("lat")
    place, core = lat // 2, lat % 2
    at_end = (place == 0) | (place == 3)

    def along_lat(pairs):
        both = [(a, b) for a, b in pairs] + [(b, a) for a, b in pairs]
        wires = [(2 * a + c, 2 * b + c) for a, b in both for c in (0, 1)]
        return lambda x: lax.ppermute(x, "lat", wires)

    even, odd, far = along_lat([(0, 1), (2, 3)]), along_lat([(1, 2)]), along_lat([(0, 3), (1, 2)])

    def across(x):
        return lax.ppermute(x, "slab", [(0, 1), (1, 0)])

    def partner(x):
        return lax.ppermute(x, "lat", [(i, i ^ 1) for i in range(8)])

    def my_half(x):
        return lax.dynamic_slice_in_dim(x, core * half, half, 1)

    def other_half(x):
        return lax.dynamic_slice_in_dim(x, (1 - core) * half, half, 1)

    own = jnp.concatenate([my_half(start_field), partner(other_half(start_field))], 0)
    regress_other = partner(regress)
    lists_other = partner(cond_lists)
    shocks = jnp.concatenate([my_half(noise), partner(other_half(noise))], 0)
    chols = jnp.concatenate([chol, partner(chol)], 0)

    def rows_of(lists):
        there = lists // (2 * blocks)
        inside = lists % (2 * blocks)
        return ((there ^ place) * 2 * blocks + ((inside // blocks) ^ core) * blocks + inside % blocks).reshape(-1)

    parts = weights(rows_of(cond_lists), regress, 2 * blocks, 0)
    parts = weights(rows_of(lists_other), regress_other, 2 * blocks, blocks, parts)
    shock = jnp.einsum("jab,jwb->jwa", chols, shocks, precision=lax.Precision.HIGHEST)

    def gathered(x):
        e1, d1 = even(x), far(x)
        o2, e2 = odd(e1), even(d1)
        return e1, d1, jnp.where(at_end, e2, o2)

    mine = lax.dynamic_slice_in_dim(own, slab * quarter, quarter, 1)
    e1, d1, s1 = gathered(mine)
    e1_x, d1_x = across(e1), across(d1)
    base = added(shock, [own], [0], parts)
    direct = added(base[:, :quarter], [e1, d1], [1, 3], parts)
    direct = added(direct, [s1], [2], parts)
    crossed = across(jnp.where(slab == 0, direct, s1))
    routed = added(base[:, quarter:], [e1_x, d1_x], [1, 3], parts)
    routed = added(routed, [crossed], [2], parts)

    f1, f2, f3 = gathered(jnp.where(slab == 0, routed, crossed))
    own_x = across(routed)
    f1_x, f2_x = across(f1), across(f2)
    direct_b = added(shock[:, :quarter], [crossed, f1], [0, 1], parts)
    direct_b = added(direct_b, [f2, f3], [3, 2], parts)
    f3_x = across(f3)
    routed_b = added(shock[:, quarter:], [own_x, f1_x, f2_x], [0, 1, 3], parts)
    routed_b = added(routed_b, [f3_x], [2], parts)

    def home(x):
        back = partner(x[blocks:])
        return x[:blocks], back

    near_a, back_a = home(jnp.where(slab == 0, direct, direct_b))
    near_b, back_b = home(jnp.where(slab == 0, routed, routed_b))
    near = jnp.concatenate([near_a, near_b], 1)
    back = jnp.concatenate([back_a, back_b], 1)
    return jnp.where(core == 0, jnp.concatenate([near, back], 1), jnp.concatenate([back, near], 1))


def solution(mesh):
    sizes = dict(mesh.shape)

    def shards(cond_lists, regress, chol, noise, start_field):
        args = (cond_lists, regress, chol, noise, start_field)
        fits = sizes["slab"] == 2 and sizes["lat"] == 8 and noise.shape[1] % 32 == 0 and noise.shape[2] % 128 == 0
        return paired(*args) if fits else general(*args)

    in_specs = (
        P(("slab", "lat"), None),
        P(("slab", "lat"), None, None),
        P(("slab", "lat"), None, None),
        P(("grp", "slab", "lat"), None, None),
        P(("grp", "lat"), None, None),
    )
    out_specs = P(("grp", "slab", "lat"), None, None)
    return jax.shard_map(shards, mesh=mesh, in_specs=in_specs, out_specs=out_specs, check_vma=False)
```

```python
import jax
import jax.numpy as jnp
from jax import lax
from jax.experimental import pallas as pl
from jax.experimental.pallas import tpu as pltpu
from jax.sharding import PartitionSpec as P


def general(cond_lists, regress, chol, noise, start_field):
    blocks, _, block_size = noise.shape
    list_length = cond_lists.shape[1]
    n_slab = lax.axis_size("slab")
    slab_pos = lax.axis_index("slab")
    factors = regress.reshape(blocks, block_size, list_length, block_size)
    shock = jnp.einsum("jab,jwb->jwa", chol, noise, precision=lax.Precision.HIGHEST)

    def step(at, carry):
        source, out = carry
        previous = lax.all_gather(source, "lat", axis=0, tiled=True)
        mean = jnp.einsum("jakb,jkwb->jwa", factors, previous[cond_lists], precision=lax.Precision.HIGHEST)
        fresh = mean + shock
        out = jnp.where(at == slab_pos, fresh, out)
        source = lax.ppermute(fresh, "slab", [(i, i + 1) for i in range(n_slab - 1)])
        return source, out

    return lax.fori_loop(0, n_slab, step, (start_field, jnp.zeros_like(noise)))[1]


IN_VMEM = pl.BlockSpec(memory_space=pltpu.VMEM)
IN_HBM = pl.BlockSpec(memory_space=pltpu.HBM)
IN_SMEM = pl.BlockSpec(memory_space=pltpu.SMEM)
PARAMS = pltpu.CompilerParams(vmem_limit_bytes=12 * 2**20)


def in_hbm(x):
    return pltpu.with_memory_space_constraint(x, pltpu.HBM)


def two_parts(x):
    high = x.astype(jnp.bfloat16)
    return high, (x - high.astype(jnp.float32)).astype(jnp.bfloat16)


def products(piece_parts, slot, part_refs, blocks, size):
    high, _, both = piece_parts
    front = high.shape[0]
    first = slot * blocks
    out = []
    high_ref, low_ref = part_refs
    columns = high_ref.shape[2]
    step = min(columns, 2 * size)
    for at in range(0, columns, step):
        w_high = high_ref[first:first + blocks, :, at:at + step].reshape(blocks * size, step)
        w_low = low_ref[first:first + blocks, :, at:at + step].reshape(blocks * size, step)
        product = jnp.dot(both, w_high, preferred_element_type=jnp.float32)
        product = product[:front] + product[front:] + jnp.dot(high, w_low, preferred_element_type=jnp.float32)
        out += [product[:, i:i + size] for i in range(0, step, size)]
    return out


def piece_parts(piece):
    high, low = two_parts(piece)
    return high, low, jnp.concatenate([high, low], axis=0)


def added(base, pieces, slots, parts):
    blocks, _, size = base.shape

    def kernel(base_ref, *refs):
        n = len(pieces)
        out_ref = refs[-1]
        total = None
        for i in range(n):
            piece = piece_parts(jnp.concatenate([refs[i][p] for p in range(blocks)], axis=1))
            terms = products(piece, slots[i], refs[n:n + 2], blocks, size)
            total = terms if total is None else [t + u for t, u in zip(total, terms)]
        for i in range(blocks):
            out_ref[i] = base_ref[i] + total[i]

    return pl.pallas_call(
        kernel,
        out_shape=jax.ShapeDtypeStruct(base.shape, jnp.float32),
        in_specs=[IN_VMEM] * (len(pieces) + 3),
        out_specs=IN_VMEM,
        compiler_params=PARAMS,
    )(base, *pieces, *parts)


def placed(turned_from, at, count, size, rows_ref, high_ref, low_ref):
    def one(k, carry):
        row = rows_ref[at * count + k]
        high, low = two_parts(turned_from(pl.ds(pl.multiple_of(k * size, size), size)).T)
        high_ref[row, :, at * size:(at + 1) * size] = high
        low_ref[row, :, at * size:(at + 1) * size] = low
        return carry

    lax.fori_loop(0, count, one, 0, unroll=4 if count % 4 == 0 else 1)


def weights(rows, regress, places):
    blocks, size, width = regress.shape
    count = width // size

    def kernel(rows_ref, regress_ref, high_ref, low_ref, buffer, arrived):
        def fetch(at):
            return pltpu.make_async_copy(regress_ref.at[at], buffer.at[at % 2], arrived.at[at % 2])

        fetch(0).start()
        high_ref[...] = jnp.zeros_like(high_ref)
        low_ref[...] = jnp.zeros_like(low_ref)
        for at in range(blocks):
            fetch(at).wait()
            if at + 1 < blocks:
                fetch(at + 1).start()
            placed(lambda ks, at=at: buffer[at % 2, :, ks], at, count, size, rows_ref, high_ref, low_ref)

    part = pltpu.VMEM((places, size, 2 * blocks * size), jnp.bfloat16)
    return pl.pallas_call(
        kernel,
        out_shape=(part,) * 2,
        in_specs=[IN_SMEM, IN_HBM],
        out_specs=(IN_VMEM,) * 2,
        scratch_shapes=[pltpu.VMEM((2, size, width), jnp.float32), pltpu.SemaphoreType.DMA((2,))],
        compiler_params=PARAMS,
        name="weights",
    )(rows, in_hbm(regress))


def weights_other(rows, parts, regress_other):
    blocks, size, width = regress_other.shape
    count = width // size

    def kernel(rows_ref, high_in, low_in, regress_ref, high_ref, low_ref):
        del high_in, low_in
        for at in range(blocks):
            placed(lambda ks, at=at: regress_ref[at, :, ks], blocks + at, count, size, rows_ref, high_ref, low_ref)

    part = pltpu.VMEM(parts[0].shape, jnp.bfloat16)
    return pl.pallas_call(
        kernel,
        out_shape=(part,) * 2,
        in_specs=[IN_SMEM] + [IN_VMEM] * 3,
        out_specs=(IN_VMEM,) * 2,
        input_output_aliases={1: 0, 2: 1},
        compiler_params=PARAMS,
        name="weights_other",
    )(rows, *parts, regress_other)


def opening(core_at, parts, chol, noise, start, chol_other, noise_other, start_other):
    blocks, nreal, size = noise.shape
    half = nreal // 2
    quarter = half // 2

    def kernel(core_ref, high_ref, low_ref, chol_hbm, noise_hbm, start_hbm, chol_o_ref, noise_o_ref, start_o_ref, *refs):
        outs, (chol_ref, noise_ref, start_ref, arrived) = refs[:4], refs[4:]
        here = pl.multiple_of(core_ref[0] * half, half)
        copies = [
            pltpu.make_async_copy(chol_hbm, chol_ref, arrived.at[0]),
            pltpu.make_async_copy(noise_hbm.at[:, pl.ds(here, half), :], noise_ref, arrived.at[1]),
            pltpu.make_async_copy(start_hbm.at[:, pl.ds(here, half), :], start_ref, arrived.at[2]),
        ]
        for copy in copies:
            copy.start()
        for copy in copies:
            copy.wait()
        own = [start_ref[i] for i in range(blocks)] + [start_o_ref[i, pl.ds(here, half), :] for i in range(blocks)]
        terms = products(piece_parts(jnp.concatenate(own, axis=1)), 0, (high_ref, low_ref), 2 * blocks, size)
        for at in range(2 * blocks):
            i = at % blocks
            high, _, both = piece_parts(noise_ref[i] if at < blocks else noise_o_ref[i, pl.ds(here, half), :])
            c_high, c_low = two_parts((chol_ref if at < blocks else chol_o_ref)[i].T)
            shock = jnp.dot(both, c_high, preferred_element_type=jnp.float32)
            shock = shock[:half] + shock[half:] + jnp.dot(high, c_low, preferred_element_type=jnp.float32)
            for q in (0, 1):
                outs[q][at] = shock[q * quarter:(q + 1) * quarter]
                outs[2 + q][at] = shock[q * quarter:(q + 1) * quarter] + terms[at][q * quarter:(q + 1) * quarter]

    piece = jax.ShapeDtypeStruct((2 * blocks, quarter, size), jnp.float32)
    held = pltpu.VMEM((blocks, half, size), jnp.float32)
    return pl.pallas_call(
        kernel,
        out_shape=(piece,) * 4,
        in_specs=[IN_SMEM] + [IN_VMEM] * 2 + [IN_HBM] * 3 + [IN_VMEM] * 3,
        out_specs=(IN_VMEM,) * 4,
        scratch_shapes=[pltpu.VMEM(chol.shape, jnp.float32), held, held, pltpu.SemaphoreType.DMA((3,))],
        compiler_params=PARAMS,
        name="opening",
    )(core_at, *parts, in_hbm(chol), in_hbm(noise), in_hbm(start), chol_other, noise_other, start_other)


def paired(cond_lists, regress, chol, noise, start_field):
    blocks, nreal, _ = noise.shape
    half, quarter = nreal // 2, nreal // 4
    slab = lax.axis_index("slab")
    lat = lax.axis_index("lat")
    place, core = lax.div(lat, 2), lax.rem(lat, 2)

    def along_lat(pairs):
        both = [(a, b) for a, b in pairs] + [(b, a) for a, b in pairs]
        wires = [(2 * a + c, 2 * b + c) for a, b in both for c in (0, 1)]
        return lambda x: lax.ppermute(x, "lat", wires)

    even, odd, far = along_lat([(0, 1), (2, 3)]), along_lat([(1, 2)]), along_lat([(0, 3), (1, 2)])

    def across(x):
        return lax.ppermute(x, "slab", [(0, 1), (1, 0)])

    def partner(x):
        return lax.ppermute(x, "lat", [(i, i ^ 1) for i in range(8)])

    start_other = partner(start_field)
    lists_other = partner(cond_lists)

    def rows_of(lists):
        there = lax.div(lists, 2 * blocks)
        inside = lax.rem(lists, 2 * blocks)
        return ((there ^ place) * (2 * blocks) + (lax.div(inside, blocks) ^ core) * blocks + lax.rem(inside, blocks)).reshape(-1)

    rows = jnp.concatenate([rows_of(cond_lists), rows_of(lists_other)])
    scalars = (slab == 0, (place == 0) | (place == 3), core == 0, core.reshape(1), core * half + slab * quarter, rows)
    scalars, start_other, regress, chol, noise = lax.optimization_barrier((scalars, start_other, regress, chol, noise))
    on_first, at_end, core_first, core_at, first, rows = scalars
    chol_other = partner(chol)
    noise_other = partner(noise)
    regress_other = partner(regress)

    mine = jnp.concatenate([lax.dynamic_slice_in_dim(x, first, quarter, 1) for x in (start_field, start_other)], 0)
    d1 = far(mine)
    e1 = even(mine)
    d1_x = across(d1)
    e2 = even(d1)
    o2 = odd(e1)
    e1_x = across(e1)
    s1 = jnp.where(at_end, e2, o2)
    parts = weights(rows, regress, 8 * blocks)
    parts = weights_other(rows, parts, regress_other)
    shock_1, shock_2, base_1, base_2 = opening(
        core_at, parts, chol, noise, start_field, chol_other, noise_other, start_other)
    direct = added(base_1, [e1, d1], [1, 3], parts)
    direct = added(direct, [s1], [2], parts)
    crossed = across(jnp.where(on_first, direct, s1))
    routed = added(base_2, [e1_x, d1_x], [1, 3], parts)
    routed = added(routed, [crossed], [2], parts)

    own_x = across(routed)
    own = jnp.where(on_first, routed, crossed)
    f2 = far(own)
    f1 = even(own)
    f2_x = across(f2)
    g2 = even(f2)
    h2 = odd(f1)
    f1_x = across(f1)
    f3 = jnp.where(at_end, g2, h2)
    f3_x = across(f3)
    direct_b = added(shock_1, [crossed, f1, f2], [0, 1, 3], parts)
    direct_b = added(direct_b, [f3], [2], parts)
    routed_b = added(shock_2, [own_x, f1_x, f2_x], [0, 1, 3], parts)
    routed_b = added(routed_b, [f3_x], [2], parts)

    def home(x):
        back = partner(x[blocks:])
        return x[:blocks], back

    near_a, back_a = home(jnp.where(on_first, direct, direct_b))
    near_b, back_b = home(jnp.where(on_first, routed, routed_b))
    near = jnp.concatenate([near_a, near_b], 1)
    back = jnp.concatenate([back_a, back_b], 1)
    return jnp.where(core_first, jnp.concatenate([near, back], 1), jnp.concatenate([back, near], 1))


def solution(mesh):
    sizes = dict(mesh.shape)

    def shards(cond_lists, regress, chol, noise, start_field):
        args = (cond_lists, regress, chol, noise, start_field)
        fits = sizes["slab"] == 2 and sizes["lat"] == 8 and noise.shape[1] % 32 == 0 and noise.shape[2] % 128 == 0
        if not fits:
            return general(*args)
        return paired(*args)

    in_specs = (
        P(("slab", "lat"), None),
        P(("slab", "lat"), None, None),
        P(("slab", "lat"), None, None),
        P(("grp", "slab", "lat"), None, None),
        P(("grp", "lat"), None, None),
    )
    out_specs = P(("grp", "slab", "lat"), None, None)
    return jax.shard_map(shards, mesh=mesh, in_specs=in_specs, out_specs=out_specs, check_vma=False)
```

```python
import jax
import jax.numpy as jnp
from jax import lax
from jax.experimental import pallas as pl
from jax.experimental.pallas import tpu as pltpu
from jax.sharding import PartitionSpec as P


def general(cond_lists, regress, chol, noise, start_field):
    blocks, _, block_size = noise.shape
    list_length = cond_lists.shape[1]
    n_slab = lax.axis_size("slab")
    slab_pos = lax.axis_index("slab")
    factors = regress.reshape(blocks, block_size, list_length, block_size)
    shock = jnp.einsum("jab,jwb->jwa", chol, noise, precision=lax.Precision.HIGHEST)

    def step(at, carry):
        source, out = carry
        previous = lax.all_gather(source, "lat", axis=0, tiled=True)
        mean = jnp.einsum("jakb,jkwb->jwa", factors, previous[cond_lists], precision=lax.Precision.HIGHEST)
        fresh = mean + shock
        out = jnp.where(at == slab_pos, fresh, out)
        source = lax.ppermute(fresh, "slab", [(i, i + 1) for i in range(n_slab - 1)])
        return source, out

    return lax.fori_loop(0, n_slab, step, (start_field, jnp.zeros_like(noise)))[1]


IN_VMEM = pl.BlockSpec(memory_space=pltpu.VMEM)
IN_HBM = pl.BlockSpec(memory_space=pltpu.HBM)
IN_SMEM = pl.BlockSpec(memory_space=pltpu.SMEM)
PARAMS = pltpu.CompilerParams(vmem_limit_bytes=12 * 2**20)


def in_hbm(x):
    return pltpu.with_memory_space_constraint(x, pltpu.HBM)


def two_parts(x):
    high = x.astype(jnp.bfloat16)
    return high, (x - high.astype(jnp.float32)).astype(jnp.bfloat16)


def products(piece_parts, slot, part_refs, blocks, size):
    high, _, both = piece_parts
    front = high.shape[0]
    first = slot * blocks
    out = []
    high_ref, low_ref = part_refs
    columns = high_ref.shape[2]
    step = min(columns, 2 * size)
    for at in range(0, columns, step):
        w_high = high_ref[first:first + blocks, :, at:at + step].reshape(blocks * size, step)
        w_low = low_ref[first:first + blocks, :, at:at + step].reshape(blocks * size, step)
        product = jnp.dot(both, w_high, preferred_element_type=jnp.float32)
        product = product[:front] + product[front:] + jnp.dot(high, w_low, preferred_element_type=jnp.float32)
        out += [product[:, i:i + size] for i in range(0, step, size)]
    return out


def piece_parts(piece):
    high, low = two_parts(piece)
    return high, low, jnp.concatenate([high, low], axis=0)


def added(base, pieces, slots, parts):
    blocks, _, size = base.shape

    def kernel(base_ref, *refs):
        n = len(pieces)
        out_ref = refs[-1]
        total = None
        for i in range(n):
            piece = piece_parts(jnp.concatenate([refs[i][p] for p in range(blocks)], axis=1))
            terms = products(piece, slots[i], refs[n:n + 2], blocks, size)
            total = terms if total is None else [t + u for t, u in zip(total, terms)]
        for i in range(blocks):
            out_ref[i] = base_ref[i] + total[i]

    return pl.pallas_call(
        kernel,
        out_shape=jax.ShapeDtypeStruct(base.shape, jnp.float32),
        in_specs=[IN_VMEM] * (len(pieces) + 3),
        out_specs=IN_VMEM,
        compiler_params=PARAMS,
    )(base, *pieces, *parts)


def placed(turned_from, at, count, size, rows_ref, high_ref, low_ref):
    def one(k, carry):
        row = rows_ref[at * count + k]
        high, low = two_parts(turned_from(pl.ds(pl.multiple_of(k * size, size), size)).T)
        high_ref[row, :, at * size:(at + 1) * size] = high
        low_ref[row, :, at * size:(at + 1) * size] = low
        return carry

    lax.fori_loop(0, count, one, 0, unroll=True)


def weights(rows, regress, places):
    blocks, size, width = regress.shape
    count = width // size

    def kernel(rows_ref, regress_ref, high_ref, low_ref, buffer, arrived):
        copies = [pltpu.make_async_copy(regress_ref.at[at], buffer.at[at], arrived.at[at]) for at in range(blocks)]
        for copy in copies:
            copy.start()
        high_ref[...] = jnp.zeros_like(high_ref)
        low_ref[...] = jnp.zeros_like(low_ref)
        for at in range(blocks):
            copies[at].wait()
            placed(lambda ks, at=at: buffer[at, :, ks], at, count, size, rows_ref, high_ref, low_ref)

    part = pltpu.VMEM((places, size, 2 * blocks * size), jnp.bfloat16)
    return pl.pallas_call(
        kernel,
        out_shape=(part,) * 2,
        in_specs=[IN_SMEM, IN_HBM],
        out_specs=(IN_VMEM,) * 2,
        scratch_shapes=[pltpu.VMEM(regress.shape, jnp.float32), pltpu.SemaphoreType.DMA((blocks,))],
        compiler_params=PARAMS,
        name="weights",
    )(rows, in_hbm(regress))


def weights_other(rows, parts, regress_other):
    blocks, size, width = regress_other.shape
    count = width // size

    def kernel(rows_ref, high_in, low_in, regress_ref, high_ref, low_ref):
        del high_in, low_in
        for at in range(blocks):
            placed(lambda ks, at=at: regress_ref[at, :, ks], blocks + at, count, size, rows_ref, high_ref, low_ref)

    part = pltpu.VMEM(parts[0].shape, jnp.bfloat16)
    return pl.pallas_call(
        kernel,
        out_shape=(part,) * 2,
        in_specs=[IN_SMEM] + [IN_VMEM] * 3,
        out_specs=(IN_VMEM,) * 2,
        input_output_aliases={1: 0, 2: 1},
        compiler_params=PARAMS,
        name="weights_other",
    )(rows, *parts, regress_other)


def opening(core_at, parts, chol, noise, start, chol_other, noise_other, start_other):
    blocks, nreal, size = noise.shape
    half = nreal // 2
    quarter = half // 2

    def kernel(core_ref, high_ref, low_ref, chol_hbm, noise_hbm, start_hbm, chol_o_ref, noise_o_ref, start_o_ref, *refs):
        outs, (chol_ref, noise_ref, start_ref, arrived) = refs[:4], refs[4:]
        here = pl.multiple_of(core_ref[0] * half, half)
        copies = [
            pltpu.make_async_copy(chol_hbm, chol_ref, arrived.at[0]),
            pltpu.make_async_copy(noise_hbm.at[:, pl.ds(here, half), :], noise_ref, arrived.at[1]),
            pltpu.make_async_copy(start_hbm.at[:, pl.ds(here, half), :], start_ref, arrived.at[2]),
        ]
        for copy in copies:
            copy.start()
        for copy in copies:
            copy.wait()
        own = [start_ref[i] for i in range(blocks)] + [start_o_ref[i, pl.ds(here, half), :] for i in range(blocks)]
        terms = products(piece_parts(jnp.concatenate(own, axis=1)), 0, (high_ref, low_ref), 2 * blocks, size)
        for at in range(2 * blocks):
            i = at % blocks
            high, _, both = piece_parts(noise_ref[i] if at < blocks else noise_o_ref[i, pl.ds(here, half), :])
            c_high, c_low = two_parts((chol_ref if at < blocks else chol_o_ref)[i].T)
            shock = jnp.dot(both, c_high, preferred_element_type=jnp.float32)
            shock = shock[:half] + shock[half:] + jnp.dot(high, c_low, preferred_element_type=jnp.float32)
            for q in (0, 1):
                outs[q][at] = shock[q * quarter:(q + 1) * quarter]
                outs[2 + q][at] = shock[q * quarter:(q + 1) * quarter] + terms[at][q * quarter:(q + 1) * quarter]

    piece = jax.ShapeDtypeStruct((2 * blocks, quarter, size), jnp.float32)
    held = pltpu.VMEM((blocks, half, size), jnp.float32)
    return pl.pallas_call(
        kernel,
        out_shape=(piece,) * 4,
        in_specs=[IN_SMEM] + [IN_VMEM] * 2 + [IN_HBM] * 3 + [IN_VMEM] * 3,
        out_specs=(IN_VMEM,) * 4,
        scratch_shapes=[pltpu.VMEM(chol.shape, jnp.float32), held, held, pltpu.SemaphoreType.DMA((3,))],
        compiler_params=PARAMS,
        name="opening",
    )(core_at, *parts, in_hbm(chol), in_hbm(noise), in_hbm(start), chol_other, noise_other, start_other)


def paired(cond_lists, regress, chol, noise, start_field):
    blocks, nreal, _ = noise.shape
    half, quarter = nreal // 2, nreal // 4
    slab = lax.axis_index("slab")
    lat = lax.axis_index("lat")
    place, core = lax.div(lat, 2), lax.rem(lat, 2)

    def along_lat(pairs):
        both = [(a, b) for a, b in pairs] + [(b, a) for a, b in pairs]
        wires = [(2 * a + c, 2 * b + c) for a, b in both for c in (0, 1)]
        return lambda x: lax.ppermute(x, "lat", wires)

    even, odd, far = along_lat([(0, 1), (2, 3)]), along_lat([(1, 2)]), along_lat([(0, 3), (1, 2)])

    def across(x):
        return lax.ppermute(x, "slab", [(0, 1), (1, 0)])

    def partner(x):
        return lax.ppermute(x, "lat", [(i, i ^ 1) for i in range(8)])

    start_other = partner(start_field)
    mine = lax.dynamic_slice_in_dim(start_field, core * half + slab * quarter, quarter, 1)
    lists_other = partner(cond_lists)

    def rows_of(lists):
        there = lax.div(lists, 2 * blocks)
        inside = lax.rem(lists, 2 * blocks)
        return ((there ^ place) * (2 * blocks) + (lax.div(inside, blocks) ^ core) * blocks + lax.rem(inside, blocks)).reshape(-1)

    rows = jnp.concatenate([rows_of(cond_lists), rows_of(lists_other)])
    scalars = (slab == 0, (place == 0) | (place == 3), core == 0, core.reshape(1), core * half + slab * quarter, rows, mine)
    scalars, start_other, regress, chol, noise = lax.optimization_barrier((scalars, start_other, regress, chol, noise))
    on_first, at_end, core_first, core_at, first, rows, mine = scalars
    chol_other = partner(chol)
    noise_other = partner(noise)
    regress_other = partner(regress)

    mine = jnp.concatenate([mine, lax.dynamic_slice_in_dim(start_other, first, quarter, 1)], 0)
    d1 = far(mine)
    e1 = even(mine)
    d1_x = across(d1)
    e2 = even(d1)
    o2 = odd(e1)
    e1_x = across(e1)
    s1 = jnp.where(at_end, e2, o2)
    parts = weights(rows, regress, 8 * blocks)
    parts = weights_other(rows, parts, regress_other)
    shock_1, shock_2, base_1, base_2 = opening(
        core_at, parts, chol, noise, start_field, chol_other, noise_other, start_other)
    direct = added(base_1, [e1, d1], [1, 3], parts)
    direct = added(direct, [s1], [2], parts)
    crossed = across(jnp.where(on_first, direct, s1))
    routed = added(base_2, [e1_x, d1_x], [1, 3], parts)
    routed = added(routed, [crossed], [2], parts)

    own_x = across(routed)
    own = jnp.where(on_first, routed, crossed)
    f2 = far(own)
    f1 = even(own)
    f2_x = across(f2)
    g2 = even(f2)
    h2 = odd(f1)
    f1_x = across(f1)
    f3 = jnp.where(at_end, g2, h2)
    f3_x = across(f3)
    direct_b = added(shock_1, [crossed, f1, f2], [0, 1, 3], parts)
    direct_b = added(direct_b, [f3], [2], parts)
    routed_b = added(shock_2, [own_x, f1_x, f2_x], [0, 1, 3], parts)
    routed_b = added(routed_b, [f3_x], [2], parts)

    def home(x):
        back = partner(x[blocks:])
        return x[:blocks], back

    near_a, back_a = home(jnp.where(on_first, direct, direct_b))
    near_b, back_b = home(jnp.where(on_first, routed, routed_b))
    near = jnp.concatenate([near_a, near_b], 1)
    back = jnp.concatenate([back_a, back_b], 1)
    return jnp.where(core_first, jnp.concatenate([near, back], 1), jnp.concatenate([back, near], 1))


def solution(mesh):
    sizes = dict(mesh.shape)

    def shards(cond_lists, regress, chol, noise, start_field):
        args = (cond_lists, regress, chol, noise, start_field)
        fits = sizes["slab"] == 2 and sizes["lat"] == 8 and noise.shape[1] % 32 == 0 and noise.shape[2] % 128 == 0
        if not fits:
            return general(*args)
        return paired(*args)

    in_specs = (
        P(("slab", "lat"), None),
        P(("slab", "lat"), None, None),
        P(("slab", "lat"), None, None),
        P(("grp", "slab", "lat"), None, None),
        P(("grp", "lat"), None, None),
    )
    out_specs = P(("grp", "slab", "lat"), None, None)
    return jax.shard_map(shards, mesh=mesh, in_specs=in_specs, out_specs=out_specs, check_vma=False)
```

```python
import jax
import jax.numpy as jnp
from jax import lax
from jax.experimental import pallas as pl
from jax.experimental.pallas import tpu as pltpu
from jax.sharding import PartitionSpec as P


def general(cond_lists, regress, chol, noise, start_field):
    blocks, _, block_size = noise.shape
    list_length = cond_lists.shape[1]
    n_slab = lax.axis_size("slab")
    slab_pos = lax.axis_index("slab")
    factors = regress.reshape(blocks, block_size, list_length, block_size)
    shock = jnp.einsum("jab,jwb->jwa", chol, noise, precision=lax.Precision.HIGHEST)

    def step(at, carry):
        source, out = carry
        previous = lax.all_gather(source, "lat", axis=0, tiled=True)
        mean = jnp.einsum("jakb,jkwb->jwa", factors, previous[cond_lists], precision=lax.Precision.HIGHEST)
        fresh = mean + shock
        out = jnp.where(at == slab_pos, fresh, out)
        source = lax.ppermute(fresh, "slab", [(i, i + 1) for i in range(n_slab - 1)])
        return source, out

    return lax.fori_loop(0, n_slab, step, (start_field, jnp.zeros_like(noise)))[1]


IN_VMEM = pl.BlockSpec(memory_space=pltpu.VMEM)
IN_HBM = pl.BlockSpec(memory_space=pltpu.HBM)
IN_SMEM = pl.BlockSpec(memory_space=pltpu.SMEM)
PARAMS = pltpu.CompilerParams(vmem_limit_bytes=12 * 2**20)


def in_hbm(x):
    return pltpu.with_memory_space_constraint(x, pltpu.HBM)


def two_parts(x):
    high = x.astype(jnp.bfloat16)
    return high, (x - high.astype(jnp.float32)).astype(jnp.bfloat16)


def products(piece_parts, slot, part_refs, blocks, size, lower=0, upper=None):
    high, _, both = piece_parts
    front = high.shape[0]
    first = slot * blocks
    out = []
    high_ref, low_ref = part_refs
    upper = high_ref.shape[2] // size if upper is None else upper
    step = (2 if (upper - lower) % 2 == 0 else 1) * size
    for at in range(lower * size, upper * size, step):
        w_high = high_ref[first:first + blocks, :, at:at + step].reshape(blocks * size, step)
        w_low = low_ref[first:first + blocks, :, at:at + step].reshape(blocks * size, step)
        product = jnp.dot(both, w_high, preferred_element_type=jnp.float32)
        product = product[:front] + product[front:] + jnp.dot(high, w_low, preferred_element_type=jnp.float32)
        out += [product[:, i:i + size] for i in range(0, step, size)]
    return out


def piece_parts(piece):
    high, low = two_parts(piece)
    return high, low, jnp.concatenate([high, low], axis=0)


def added(base, pieces, slots, parts, lower=0, upper=None, unless=None):
    blocks, front, size = base.shape
    upper = blocks if upper is None else upper
    unless = () if unless is None else unless

    def kernel(base_ref, *refs):
        n = len(pieces)
        out_ref = refs[-1]
        total = None
        for i in range(n):
            piece = piece_parts(jnp.concatenate([refs[i][p] for p in range(blocks)], axis=1))
            terms = products(piece, slots[i], refs[n:n + 2], blocks, size, lower, upper)
            total = terms if total is None else [t + u for t, u in zip(total, terms)]
        for i in range(upper - lower):
            value = base_ref[lower + i] + total[i]
            out_ref[i] = jnp.where(refs[n + 2][0] != 0, refs[n + 3][lower + i], value) if unless else value

    return pl.pallas_call(
        kernel,
        out_shape=jax.ShapeDtypeStruct((upper - lower, front, size), jnp.float32),
        in_specs=[IN_VMEM] * (len(pieces) + 3) + [IN_SMEM, IN_VMEM][:len(unless)],
        out_specs=IN_VMEM,
        compiler_params=PARAMS,
    )(base, *pieces, *parts, *unless)


def stored(core_at, near, back, which, nreal, earlier=()):
    blocks, quarter, size = near.shape
    half = nreal // 2

    def kernel(core_ref, near_ref, back_ref, *refs):
        out_ref, sent = refs[-2:]
        core = core_ref[0]
        copies = []
        for i, (ref, side) in enumerate(((near_ref, core), (back_ref, 1 - core))):
            rows = pl.ds(pl.multiple_of(side * half + which * quarter, quarter), quarter)
            copies.append(pltpu.make_async_copy(ref, out_ref.at[:, rows, :], sent.at[i]))
        for copy in copies:
            copy.start()
        for copy in copies:
            copy.wait()

    return pl.pallas_call(
        kernel,
        out_shape=pltpu.HBM((blocks, nreal, size), jnp.float32),
        in_specs=[IN_SMEM] + [IN_VMEM] * 2 + [IN_HBM] * len(earlier),
        out_specs=IN_HBM,
        scratch_shapes=[pltpu.SemaphoreType.DMA((2,))],
        input_output_aliases={3: 0} if earlier else {},
        compiler_params=PARAMS,
    )(core_at, near, back, *earlier)


def placed(turned_from, at, count, size, rows_ref, high_ref, low_ref):
    def one(k, carry):
        row = rows_ref[at * count + k]
        high, low = two_parts(turned_from(pl.ds(pl.multiple_of(k * size, size), size)).T)
        high_ref[row, :, at * size:(at + 1) * size] = high
        low_ref[row, :, at * size:(at + 1) * size] = low
        return carry

    lax.fori_loop(0, count, one, 0, unroll=True)


def weights(rows, regress, places):
    blocks, size, width = regress.shape
    count = width // size

    def kernel(rows_ref, regress_ref, high_ref, low_ref, buffer, arrived):
        copies = [pltpu.make_async_copy(regress_ref.at[at], buffer.at[at], arrived.at[at]) for at in range(blocks)]
        for copy in copies:
            copy.start()
        high_ref[...] = jnp.zeros_like(high_ref)
        low_ref[...] = jnp.zeros_like(low_ref)
        for at in range(blocks):
            copies[at].wait()
            placed(lambda ks, at=at: buffer[at, :, ks], at, count, size, rows_ref, high_ref, low_ref)

    part = pltpu.VMEM((places, size, 2 * blocks * size), jnp.bfloat16)
    return pl.pallas_call(
        kernel,
        out_shape=(part,) * 2,
        in_specs=[IN_SMEM, IN_HBM],
        out_specs=(IN_VMEM,) * 2,
        scratch_shapes=[pltpu.VMEM(regress.shape, jnp.float32), pltpu.SemaphoreType.DMA((blocks,))],
        compiler_params=PARAMS,
        name="weights",
    )(rows, in_hbm(regress))


def weights_other(rows, parts, regress_other):
    blocks, size, width = regress_other.shape
    count = width // size

    def kernel(rows_ref, high_in, low_in, regress_ref, high_ref, low_ref):
        del high_in, low_in
        for at in range(blocks):
            placed(lambda ks, at=at: regress_ref[at, :, ks], blocks + at, count, size, rows_ref, high_ref, low_ref)

    part = pltpu.VMEM(parts[0].shape, jnp.bfloat16)
    return pl.pallas_call(
        kernel,
        out_shape=(part,) * 2,
        in_specs=[IN_SMEM] + [IN_VMEM] * 3,
        out_specs=(IN_VMEM,) * 2,
        input_output_aliases={1: 0, 2: 1},
        compiler_params=PARAMS,
        name="weights_other",
    )(rows, *parts, regress_other)


def opening(core_at, parts, chol, noise, start, chol_other, noise_other, start_other):
    blocks, nreal, size = noise.shape
    half = nreal // 2
    quarter = half // 2

    def kernel(core_ref, high_ref, low_ref, chol_hbm, noise_hbm, start_hbm, chol_o_ref, noise_o_ref, start_o_ref, *refs):
        outs, (chol_ref, noise_ref, start_ref, arrived) = refs[:4], refs[4:]
        here = pl.multiple_of(core_ref[0] * half, half)
        copies = [
            pltpu.make_async_copy(chol_hbm, chol_ref, arrived.at[0]),
            pltpu.make_async_copy(noise_hbm.at[:, pl.ds(here, half), :], noise_ref, arrived.at[1]),
            pltpu.make_async_copy(start_hbm.at[:, pl.ds(here, half), :], start_ref, arrived.at[2]),
        ]
        for copy in copies:
            copy.start()
        for copy in copies:
            copy.wait()
        own = [start_ref[i] for i in range(blocks)] + [start_o_ref[i, pl.ds(here, half), :] for i in range(blocks)]
        terms = products(piece_parts(jnp.concatenate(own, axis=1)), 0, (high_ref, low_ref), 2 * blocks, size)
        for at in range(2 * blocks):
            i = at % blocks
            high, _, both = piece_parts(noise_ref[i] if at < blocks else noise_o_ref[i, pl.ds(here, half), :])
            c_high, c_low = two_parts((chol_ref if at < blocks else chol_o_ref)[i].T)
            shock = jnp.dot(both, c_high, preferred_element_type=jnp.float32)
            shock = shock[:half] + shock[half:] + jnp.dot(high, c_low, preferred_element_type=jnp.float32)
            for q in (0, 1):
                outs[q][at] = shock[q * quarter:(q + 1) * quarter]
                outs[2 + q][at] = shock[q * quarter:(q + 1) * quarter] + terms[at][q * quarter:(q + 1) * quarter]

    piece = jax.ShapeDtypeStruct((2 * blocks, quarter, size), jnp.float32)
    held = pltpu.VMEM((blocks, half, size), jnp.float32)
    return pl.pallas_call(
        kernel,
        out_shape=(piece,) * 4,
        in_specs=[IN_SMEM] + [IN_VMEM] * 2 + [IN_HBM] * 3 + [IN_VMEM] * 3,
        out_specs=(IN_VMEM,) * 4,
        scratch_shapes=[pltpu.VMEM(chol.shape, jnp.float32), held, held, pltpu.SemaphoreType.DMA((3,))],
        compiler_params=PARAMS,
        name="opening",
    )(core_at, *parts, in_hbm(chol), in_hbm(noise), in_hbm(start), chol_other, noise_other, start_other)


def paired(cond_lists, regress, chol, noise, start_field):
    blocks, nreal, _ = noise.shape
    half, quarter = nreal // 2, nreal // 4
    slab = lax.axis_index("slab")
    lat = lax.axis_index("lat")
    place, core = lax.div(lat, 2), lax.rem(lat, 2)

    def along_lat(pairs):
        both = [(a, b) for a, b in pairs] + [(b, a) for a, b in pairs]
        wires = [(2 * a + c, 2 * b + c) for a, b in both for c in (0, 1)]
        return lambda x: lax.ppermute(x, "lat", wires)

    even, odd, far = along_lat([(0, 1), (2, 3)]), along_lat([(1, 2)]), along_lat([(0, 3), (1, 2)])

    def across(x):
        return lax.ppermute(x, "slab", [(0, 1), (1, 0)])

    def partner(x):
        return lax.ppermute(x, "lat", [(i, i ^ 1) for i in range(8)])

    start_other = partner(start_field)
    mine = lax.dynamic_slice_in_dim(start_field, core * half + slab * quarter, quarter, 1)
    lists_other = partner(cond_lists)

    def rows_of(lists):
        there = lax.div(lists, 2 * blocks)
        inside = lax.rem(lists, 2 * blocks)
        return ((there ^ place) * (2 * blocks) + (lax.div(inside, blocks) ^ core) * blocks + lax.rem(inside, blocks)).reshape(-1)

    rows = jnp.concatenate([rows_of(cond_lists), rows_of(lists_other)])
    scalars = (slab == 0, (slab == 0).astype(jnp.int32).reshape(1), (place == 0) | (place == 3), core.reshape(1), core * half + slab * quarter, rows, mine)
    scalars, start_other, regress, chol, noise = lax.optimization_barrier((scalars, start_other, regress, chol, noise))
    on_first, first_at, at_end, core_at, first, rows, mine = scalars
    chol_other = partner(chol)
    noise_other = partner(noise)
    regress_other = partner(regress)

    mine = jnp.concatenate([mine, lax.dynamic_slice_in_dim(start_other, first, quarter, 1)], 0)
    d1 = far(mine)
    e1 = even(mine)
    d1_x = across(d1)
    e2 = even(d1)
    o2 = odd(e1)
    e1_x = across(e1)
    s1 = jnp.where(at_end, e2, o2)
    parts = weights(rows, regress, 8 * blocks)
    parts = weights_other(rows, parts, regress_other)
    shock_1, shock_2, base_1, base_2 = opening(
        core_at, parts, chol, noise, start_field, chol_other, noise_other, start_other)
    direct = added(base_1, [e1, d1], [1, 3], parts)
    direct = added(direct, [s1], [2], parts)
    crossed = across(jnp.where(on_first, direct, s1))
    routed = added(base_2, [e1_x, d1_x], [1, 3], parts)
    routed = added(routed, [crossed], [2], parts)

    own_x = across(routed)
    own = jnp.where(on_first, routed, crossed)
    f2 = far(own)
    f1 = even(own)
    f2_x = across(f2)
    g2 = even(f2)
    h2 = odd(f1)
    f1_x = across(f1)
    f3 = jnp.where(at_end, g2, h2)
    f3_x = across(f3)
    direct_b = added(shock_1, [crossed, f1, f2], [0, 1, 3], parts)
    direct_b = added(direct_b, [f3], [2], parts)
    routed_b = added(shock_2, [own_x, f1_x, f2_x], [0, 1, 3], parts)
    near_a = jnp.where(on_first, direct[:blocks], direct_b[:blocks])
    back_a = partner(jnp.where(on_first, direct[blocks:], direct_b[blocks:]))
    out = stored(core_at, near_a, back_a, 0, nreal)
    far_b = added(routed_b, [f3_x], [2], parts, blocks, 2 * blocks, (first_at, routed))
    back_b = partner(far_b)
    near_b = added(routed_b, [f3_x], [2], parts, 0, blocks, (first_at, routed))
    return stored(core_at, near_b, back_b, 1, nreal, (out,))


def solution(mesh):
    sizes = dict(mesh.shape)

    def shards(cond_lists, regress, chol, noise, start_field):
        args = (cond_lists, regress, chol, noise, start_field)
        fits = sizes["slab"] == 2 and sizes["lat"] == 8 and noise.shape[1] % 32 == 0 and noise.shape[2] % 128 == 0
        if not fits:
            return general(*args)
        return paired(*args)

    in_specs = (
        P(("slab", "lat"), None),
        P(("slab", "lat"), None, None),
        P(("slab", "lat"), None, None),
        P(("grp", "slab", "lat"), None, None),
        P(("grp", "lat"), None, None),
    )
    out_specs = P(("grp", "slab", "lat"), None, None)
    return jax.shard_map(shards, mesh=mesh, in_specs=in_specs, out_specs=out_specs, check_vma=False)
```
